32 devices in a mesh: row: 4 (over y, core), col: 8 (over z, x).
Axes of the slice: x: 2, y: 2, z: 4, core: 2. Of those that a mesh axis runs over, the one named last changes fastest.
Arguments:
- coords: float32 [64, 16384], P(None, ('row', 'col')), may hold values from -6 to 6
- dissimilarity: float32 [16384, 8192], P('row', 'col'), as said below
Outputs:
- updated: float32 [64, 16384], P(None, ('row', 'col'))
The draws below stay inside these ranges and needn't reach their ends.
Inputs may be any that keep to these rules, and one draw needn't show every extreme that they name: `dissimilarity`: each unordered pair of distinct samples appears in exactly one entry, placed as the steps state; the entries that name no pair are positive too.
All inputs are finite; a program needn't handle non-finite values.
Results may differ from the reference program's by a relative error of at most 0.0003.
Values sent between devices are 32-bit elements; how exact they have to be, the bound alone decides.
A program may use at most 128 MiB of HBM per device.

```python
import math
import jax
import jax.numpy as jnp
from jax import lax

DIMS = 64
COLS = 2048
ITERS = 2
SAMPLES = 16384


def latent_spacing(leading, trailing):
    inner_prod = jnp.dot(leading.T, trailing, precision=lax.Precision.HIGHEST)
    leading_norms = jnp.sum(leading * leading, axis=0)
    trailing_norms = jnp.sum(trailing * trailing, axis=0)
    return jnp.sqrt(jnp.maximum(leading_norms[:, None] + trailing_norms[None, :] - 2.0 * inner_prod, 0.0) + 1.0)


def draw_dissimilarity(key, part):
    latent_key = jax.random.fold_in(key, 21)
    jitter_key = jax.random.fold_in(key, 22)
    block_count = SAMPLES // COLS
    half_width = COLS // 2
    latent = jax.random.normal(latent_key, (DIMS, SAMPLES), jnp.float32)
    weights = jnp.ones((SAMPLES,), jnp.float32)
    grouped = latent.reshape(DIMS, block_count, COLS)
    grouped_weights = weights.reshape(block_count, COLS)
    row_iota = lax.broadcasted_iota(jnp.int32, (COLS, half_width), 0)
    col_iota = lax.broadcasted_iota(jnp.int32, (COLS, half_width), 1)

    def one_row(row_index):
        rows_coords = lax.dynamic_index_in_dim(grouped, row_index, 1, keepdims=False)
        rows_weights = lax.dynamic_index_in_dim(grouped_weights, row_index, 0, keepdims=False)

        def one_tile(col_index):
            cols_coords = lax.dynamic_index_in_dim(grouped, col_index, 1, keepdims=False)
            cols_weights = lax.dynamic_index_in_dim(grouped_weights, col_index, 0, keepdims=False)
            row_first = row_index <= col_index
            offset = jnp.where(row_first, 0, half_width).astype(jnp.int32)
            leading = jnp.where(row_first, rows_coords, cols_coords)
            trailing = lax.dynamic_slice_in_dim(jnp.where(row_first, cols_coords, rows_coords), offset, half_width, 1)
            leading_weights = jnp.where(row_first, rows_weights, cols_weights)
            trailing_weights = lax.dynamic_slice_in_dim(jnp.where(row_first, cols_weights, rows_weights), offset, half_width, 0)
            scaled = latent_spacing(leading, trailing) * jnp.sqrt(leading_weights[:, None] * trailing_weights[None, :])
            late_coords = rows_coords[:, half_width:]
            late_weights = rows_weights[half_width:]
            late = latent_spacing(late_coords, late_coords) * jnp.sqrt(late_weights[:, None] * late_weights[None, :])
            late_full = jnp.concatenate([late, jnp.zeros_like(late)], axis=0)
            swap_mask = (row_index == col_index) & (row_iota < half_width) & (col_iota < row_iota)
            base = jnp.where(swap_mask, late_full, scaled)
            jitter = jax.random.uniform(jax.random.fold_in(jitter_key, row_index * block_count + col_index), (COLS, half_width), jnp.float32)
            return base * jnp.exp(math.log(2.0) * (2.0 * jitter - 1.0))
        return lax.map(one_tile, jnp.arange(block_count, dtype=jnp.int32))
    stacked = lax.map(one_row, jnp.arange(block_count, dtype=jnp.int32))
    return stacked.transpose(0, 2, 1, 3).reshape(SAMPLES, SAMPLES // 2).astype(jnp.float32)


def levels(own_key, dims, cuts, smallest, high):
    def one(axis_at, parts):
        heights = jax.random.uniform(jax.random.fold_in(jax.random.fold_in(own_key, 6), axis_at), (parts,), jnp.float32, smallest / len(cuts), high / len(cuts))
        return jnp.repeat(jnp.exp(heights), dims[axis_at] // parts).reshape((-1,) + (1,) * (len(dims) - axis_at - 1))

    factor_of = one(*cuts[0])
    for cut in cuts[1:]:
        factor_of = factor_of * one(*cut)
    return factor_of


def scatter_about(stream_key, dims, width, most, pieces=(), held_as=jnp.bfloat16):
    gain = levels(stream_key, dims, pieces, -0.22, 0.18) if pieces else 1.0
    drawn = jax.random.normal(stream_key, dims, jnp.float32) * width * gain
    return jnp.minimum(jnp.maximum(drawn, -most), most).astype(held_as)


def setup_inputs(seed: int = 0) -> dict:
    key_of = jax.random.split(jax.random.key(seed), 3)
    coords = scatter_about(key_of[0], (DIMS, SAMPLES), 1.0, 6.0, ((1, 32),), jnp.float32)
    dissimilarity = draw_dissimilarity(jax.random.fold_in(key_of[2], 71), 0)
    return dict(coords=coords, dissimilarity=dissimilarity)


def compute_ratios(values, leading, trailing):
    inner_prod = lax.dot_general(leading, trailing, (((0,), (0,)), ((), ())), precision=lax.Precision.HIGHEST, preferred_element_type=jnp.float32)
    leading_norms = lax.optimization_barrier(jnp.sum(leading * leading, axis=0))
    trailing_norms = lax.optimization_barrier(jnp.sum(trailing * trailing, axis=0))
    spacing = jnp.sqrt(leading_norms[:, None] + trailing_norms[None, :] - 2.0 * inner_prod + 1.0)
    return values / spacing

def pair_terms(leading, trailing, ratios):
    pulled = lax.dot_general(trailing, ratios, (((1,), (1,)), ((), ())), precision=lax.Precision.HIGHEST, preferred_element_type=jnp.float32)
    pushed = lax.dot_general(leading, ratios, (((1,), (0,)), ((), ())), precision=lax.Precision.HIGHEST, preferred_element_type=jnp.float32)
    leading_terms = leading * lax.optimization_barrier(jnp.sum(ratios, axis=1))[None, :] - pulled
    trailing_terms = trailing * lax.optimization_barrier(jnp.sum(ratios, axis=0))[None, :] - pushed
    return (leading_terms, trailing_terms)

def offdiagonal_terms(values, rows_coords, cols_coords, row_first):
    half_width = values.shape[1]
    leading = jnp.where(row_first, rows_coords, cols_coords)
    partner = jnp.where(row_first, cols_coords, rows_coords)
    offset = jnp.where(row_first, 0, half_width).astype(jnp.int32)
    trailing = lax.dynamic_slice_in_dim(partner, offset, half_width, 1)
    ratios = compute_ratios(values, leading, trailing)
    leading_terms, trailing_terms = pair_terms(leading, trailing, ratios)
    placed = lax.dynamic_update_slice_in_dim(jnp.zeros_like(partner), trailing_terms, offset, 1)
    return (jnp.where(row_first, leading_terms, placed), jnp.where(row_first, placed, leading_terms))

def diagonal_terms(values, rows_coords, cols_coords, row_first):
    half_width = values.shape[1]
    first_half = rows_coords[:, :half_width]
    second_half = rows_coords[:, half_width:]
    upper_values = values[:half_width]
    lower_values = values[half_width:]
    row_iota = lax.broadcasted_iota(jnp.int32, (half_width, half_width), 0)
    col_iota = lax.broadcasted_iota(jnp.int32, (half_width, half_width), 1)
    cross = compute_ratios(lower_values, second_half, first_half)
    cross_second, cross_first = pair_terms(second_half, first_half, cross)
    early = jnp.where(col_iota > row_iota, compute_ratios(upper_values, first_half, first_half), 0.0)
    late = jnp.where(col_iota < row_iota, compute_ratios(upper_values, second_half, second_half), 0.0)
    early_rows, early_cols = pair_terms(first_half, first_half, early)
    late_rows, late_cols = pair_terms(second_half, second_half, late)
    row_share = jnp.concatenate([early_rows + early_cols + cross_first, late_rows + late_cols + cross_second], axis=1)
    return (row_share, jnp.zeros_like(row_share))

def tile_terms(values, rows_coords, cols_coords, row_index, col_index):
    return lax.cond(row_index == col_index, diagonal_terms, offdiagonal_terms, values, rows_coords, cols_coords, row_index < col_index)

def reference(coords, dissimilarity):
    sample_count = coords.shape[1]
    block_count = sample_count // COLS
    half_width = COLS // 2
    tiles = dissimilarity.reshape(block_count, COLS, block_count, half_width)
    current = coords
    for iteration in range(ITERS):
        grouped = current.reshape(DIMS, block_count, COLS)

        def one_row(partials, row_index):
            rows_coords = lax.dynamic_index_in_dim(grouped, row_index, 1, keepdims=False)
            row_tiles = lax.dynamic_index_in_dim(tiles, row_index, 0, keepdims=False)

            def one_tile(col_index):
                values = lax.dynamic_index_in_dim(row_tiles, col_index, 1, keepdims=False)
                cols_coords = lax.dynamic_index_in_dim(grouped, col_index, 1, keepdims=False)
                return tile_terms(values, rows_coords, cols_coords, row_index, col_index)
            row_shares, col_shares = lax.map(one_tile, jnp.arange(block_count, dtype=jnp.int32))
            partials = partials + jnp.transpose(col_shares, (1, 0, 2))
            own_row = lax.dynamic_index_in_dim(partials, row_index, 1, keepdims=False) + lax.optimization_barrier(jnp.sum(row_shares, axis=0))
            partials = lax.dynamic_update_index_in_dim(partials, own_row, row_index, 1)
            return (partials, None)
        initial = jnp.zeros((DIMS, block_count, COLS), jnp.float32)
        summed, _ = lax.scan(one_row, initial, jnp.arange(block_count, dtype=jnp.int32))
        current = summed.reshape(DIMS, sample_count) / sample_count
    return current
```

```python
import functools

import jax
import jax.numpy as jnp
from jax import lax
from jax.experimental import pallas as pl
from jax.experimental.pallas import tpu as pltpu
from jax.sharding import PartitionSpec as P

ITERS = 2
STEP_ROWS = 512


def from_root(value, axis, source):
    kept = jnp.where(lax.axis_index(axis) == source, value, 0).astype(value.dtype)
    return lax.psum(kept, axis)


def terms_kernel(
    per_root, tile_count, x_ref, delta_ref, out_ref,
    lead_ref, pull_ref, trail_ref, push_ref, norm_col, norm_row, xt_ref, acc_t, acc,
):
    half = delta_ref.shape[1]
    block = 2 * half
    dims, count = x_ref.shape
    rows = delta_ref.shape[0]
    cols_at = tile_count * block
    step = pl.program_id(0)
    row_pos = lax.axis_index("row")
    col_pos = lax.axis_index("col")
    bf16, f32 = jnp.bfloat16, jnp.float32
    piece = 512

    @pl.when(step == 0)
    def _prepare():
        @pl.loop(0, count // piece)
        def _(k):
            at = pl.ds(pl.multiple_of(k * piece, piece), piece)
            x = x_ref[:, at]
            hi = x.astype(bf16).astype(f32)
            lo = (x - hi).astype(bf16).astype(f32)
            kept = hi + lo
            norm_row[:, at] = jnp.broadcast_to(
                jnp.sum(kept * kept, axis=0, keepdims=True), (8, piece)
            )
            stack = jnp.concatenate([hi, lo], axis=0)
            trail_ref[:, at] = jnp.concatenate([hi, hi, lo, lo], axis=0).astype(bf16) * -2.0
            push_ref[:, at] = jnp.concatenate(
                [hi, lo, jnp.ones((16, piece), f32)], axis=0
            ).astype(bf16)
            flipped = stack.T
            xt = flipped[:, :dims] + flipped[:, dims:]
            xt_ref[at, :] = xt
            norm_col[at, :] = jnp.sum(xt * xt, axis=1, keepdims=True) + 1.0
            pieces = flipped.astype(bf16)
            lead_ref[at, :] = jnp.concatenate([pieces, pieces], axis=1)
            pull_ref[at, :] = jnp.concatenate([pieces, jnp.ones_like(pieces)], axis=1)
            acc_t[at, :] = jnp.zeros((piece, dims), f32)
            acc[:, at] = jnp.zeros((dims, piece), f32)

    def spacing(lead, trail):
        gram = jnp.dot(lead_ref[lead, :], trail_ref[:, trail], preferred_element_type=f32)
        return gram + (norm_col[lead, :] + norm_row[0:1, trail])

    def add_terms(lead, trail, ratios):
        ratios = ratios.astype(bf16)
        pulled = jnp.dot(ratios, pull_ref[trail, :], preferred_element_type=f32)
        acc_t[lead, :] += xt_ref[lead, :] * pulled[:, 2 * dims:3 * dims] - (
            pulled[:, :dims] + pulled[:, dims:2 * dims]
        )
        pushed = jnp.dot(push_ref[:, lead], ratios, preferred_element_type=f32)
        acc[:, trail] += x_ref[:, trail] * pushed[2 * dims:2 * dims + 1, :] - (
            pushed[:dims, :] + pushed[dims:2 * dims, :]
        )

    steps_per_tile = block // rows
    slot = step // steps_per_tile
    first = (step % steps_per_tile) * rows
    row_index = row_pos * per_root + slot
    upper = (row_index == col_pos) & (first < half)
    slot_at = slot * block

    @pl.when(jnp.logical_not(upper))
    def _plain():
        lead_at = jnp.where(row_index > col_pos, cols_at, slot_at) + first
        trail_at = jnp.where(
            row_index < col_pos, cols_at,
            jnp.where(row_index > col_pos, slot_at + half, slot_at),
        )
        lead = pl.ds(pl.multiple_of(lead_at, rows), rows)
        trail = pl.ds(pl.multiple_of(trail_at, half), half)
        add_terms(lead, trail, delta_ref[...] * lax.rsqrt(spacing(lead, trail)))

    @pl.when(upper)
    def _split():
        early_lead = pl.ds(pl.multiple_of(slot_at + first, rows), rows)
        early_trail = pl.ds(pl.multiple_of(slot_at, half), half)
        late_lead = pl.ds(pl.multiple_of(slot_at + half + first, rows), rows)
        late_trail = pl.ds(pl.multiple_of(slot_at + half, half), half)
        row_iota = first + lax.broadcasted_iota(jnp.int32, (rows, half), 0)
        col_iota = lax.broadcasted_iota(jnp.int32, (rows, half), 1)
        early = jnp.where(
            col_iota > row_iota,
            delta_ref[...] * lax.rsqrt(spacing(early_lead, early_trail)), 0.0,
        )
        add_terms(early_lead, early_trail, early)
        late = jnp.where(
            col_iota < row_iota,
            delta_ref[...] * lax.rsqrt(spacing(late_lead, late_trail)), 0.0,
        )
        add_terms(late_lead, late_trail, late)

    @pl.when(step == pl.num_programs(0) - 1)
    def _finish():
        @pl.loop(0, count // piece)
        def _(k):
            at = pl.ds(pl.multiple_of(k * piece, piece), piece)
            out_ref[:, at] = acc[:, at] + acc_t[at, :].T


def local_terms(x, dissimilarity, per_root):
    dims, count = x.shape
    height, half = dissimilarity.shape
    tile_count = height // (2 * half)
    bf16, f32 = jnp.bfloat16, jnp.float32
    whole = pl.BlockSpec(memory_space=pltpu.VMEM)
    return pl.pallas_call(
        functools.partial(terms_kernel, per_root, tile_count),
        grid=(height // STEP_ROWS,),
        out_shape=jax.ShapeDtypeStruct((dims, count), f32),
        in_specs=[whole, pl.BlockSpec((STEP_ROWS, half), lambda i: (i, 0))],
        out_specs=whole,
        scratch_shapes=[
            pltpu.VMEM((count, 4 * dims), bf16),
            pltpu.VMEM((count, 4 * dims), bf16),
            pltpu.VMEM((4 * dims, count), bf16),
            pltpu.VMEM((2 * dims + 16, count), bf16),
            pltpu.VMEM((count, 1), f32),
            pltpu.VMEM((8, count), f32),
            pltpu.VMEM((count, dims), f32),
            pltpu.VMEM((count, dims), f32),
            pltpu.VMEM((dims, count), f32),
        ],
        compiler_params=pltpu.CompilerParams(vmem_limit_bytes=56 * 1024 * 1024),
    )(x, dissimilarity)


def local(coords, dissimilarity):
    half_width = dissimilarity.shape[1]
    block_width = 2 * half_width
    per_root = lax.axis_size("col") // lax.axis_size("row")
    inverse_count = 1.0 / (block_width * lax.axis_size("col"))
    row_pos = lax.axis_index("row")
    col_pos = lax.axis_index("col")
    own_width = coords.shape[1]
    column_offset = col_pos % per_root * block_width
    at_root = row_pos == col_pos // per_root
    current = coords
    for iteration in range(ITERS):
        rows_coords = lax.all_gather(current, "col", axis=1, tiled=True)
        height = rows_coords.shape[1]
        root_piece = lax.dynamic_slice_in_dim(rows_coords, column_offset, block_width, 1)
        cols_coords = from_root(root_piece, "row", col_pos // per_root)
        both = jnp.concatenate([rows_coords, cols_coords], axis=1)
        parts = local_terms(both, dissimilarity, per_root)
        row_part, col_part = parts[:, :height], parts[:, height:]
        col_total = lax.psum(col_part, "row")
        placed = lax.dynamic_update_slice_in_dim(
            jnp.zeros_like(row_part), col_total, column_offset, 1
        )
        row_part = row_part + jnp.where(at_root, placed, 0.0)
        current = lax.psum_scatter(row_part, "col", scatter_dimension=1, tiled=True) * inverse_count
    return current


def solution(mesh):
    in_specs = (P(None, ("row", "col")), P("row", "col"))
    out_specs = P(None, ("row", "col"))
    return jax.shard_map(local, mesh=mesh, in_specs=in_specs, out_specs=out_specs, check_vma=False)
```

```python
import functools

import jax
import jax.numpy as jnp
from jax import lax
from jax.experimental import pallas as pl
from jax.experimental.pallas import tpu as pltpu
from jax.sharding import PartitionSpec as P

ITERS = 2
STEP_ROWS = 512


def terms_kernel(
    per_root, tile_count, x_ref, delta_ref, out_ref,
    lead_ref, pull_ref, trail_ref, push_ref, norm_col, norm_row, xt_ref, acc_t, acc,
):
    half = delta_ref.shape[1]
    block = 2 * half
    dims, count = x_ref.shape
    rows = delta_ref.shape[0]
    cols_at = tile_count * block
    step = pl.program_id(0)
    row_pos = lax.axis_index("row")
    col_pos = lax.axis_index("col")
    bf16, f32 = jnp.bfloat16, jnp.float32
    piece = 512

    @pl.when(step == 0)
    def _prepare():
        @pl.loop(0, count // piece)
        def _(k):
            at = pl.ds(pl.multiple_of(k * piece, piece), piece)
            x = x_ref[:, at]
            hi = x.astype(bf16).astype(f32)
            lo = (x - hi).astype(bf16).astype(f32)
            kept = hi + lo
            norm_row[:, at] = jnp.broadcast_to(
                jnp.sum(kept * kept, axis=0, keepdims=True), (8, piece)
            )
            stack = jnp.concatenate([hi, lo], axis=0)
            trail_ref[:, at] = jnp.concatenate([hi, hi, lo, lo], axis=0).astype(bf16) * -2.0
            push_ref[:, at] = jnp.concatenate(
                [hi, lo, jnp.ones((16, piece), f32)], axis=0
            ).astype(bf16)
            flipped = stack.T
            xt = flipped[:, :dims] + flipped[:, dims:]
            xt_ref[at, :] = xt
            norm_col[at, :] = jnp.sum(xt * xt, axis=1, keepdims=True) + 1.0
            pieces = flipped.astype(bf16)
            lead_ref[at, :] = jnp.concatenate([pieces, pieces], axis=1)
            pull_ref[at, :] = jnp.concatenate([pieces, jnp.ones_like(pieces)], axis=1)
            acc_t[at, :] = jnp.zeros((piece, dims), f32)
            acc[:, at] = jnp.zeros((dims, piece), f32)

    def spacing(lead, trail):
        gram = jnp.dot(lead_ref[lead, :], trail_ref[:, trail], preferred_element_type=f32)
        return gram + (norm_col[lead, :] + norm_row[0:1, trail])

    def add_terms(lead, trail, ratios):
        ratios = ratios.astype(bf16)
        pulled = jnp.dot(ratios, pull_ref[trail, :], preferred_element_type=f32)
        acc_t[lead, :] += xt_ref[lead, :] * pulled[:, 2 * dims:3 * dims] - (
            pulled[:, :dims] + pulled[:, dims:2 * dims]
        )
        pushed = jnp.dot(push_ref[:, lead], ratios, preferred_element_type=f32)
        acc[:, trail] += x_ref[:, trail] * pushed[2 * dims:2 * dims + 1, :] - (
            pushed[:dims, :] + pushed[dims:2 * dims, :]
        )

    steps_per_tile = block // rows
    slot = step // steps_per_tile
    first = (step % steps_per_tile) * rows
    row_index = row_pos * per_root + slot
    upper = (row_index == col_pos) & (first < half)
    slot_at = slot * block

    @pl.when(jnp.logical_not(upper))
    def _plain():
        lead_at = jnp.where(row_index > col_pos, cols_at, slot_at) + first
        trail_at = jnp.where(
            row_index < col_pos, cols_at,
            jnp.where(row_index > col_pos, slot_at + half, slot_at),
        )
        lead = pl.ds(pl.multiple_of(lead_at, rows), rows)
        trail = pl.ds(pl.multiple_of(trail_at, half), half)
        add_terms(lead, trail, delta_ref[...] * lax.rsqrt(spacing(lead, trail)))

    @pl.when(upper)
    def _split():
        early_lead = pl.ds(pl.multiple_of(slot_at + first, rows), rows)
        early_trail = pl.ds(pl.multiple_of(slot_at, half), half)
        late_lead = pl.ds(pl.multiple_of(slot_at + half + first, rows), rows)
        late_trail = pl.ds(pl.multiple_of(slot_at + half, half), half)
        row_iota = first + lax.broadcasted_iota(jnp.int32, (rows, half), 0)
        col_iota = lax.broadcasted_iota(jnp.int32, (rows, half), 1)
        early = jnp.where(
            col_iota > row_iota,
            delta_ref[...] * lax.rsqrt(spacing(early_lead, early_trail)), 0.0,
        )
        add_terms(early_lead, early_trail, early)
        late = jnp.where(
            col_iota < row_iota,
            delta_ref[...] * lax.rsqrt(spacing(late_lead, late_trail)), 0.0,
        )
        add_terms(late_lead, late_trail, late)

    @pl.when(step == pl.num_programs(0) - 1)
    def _finish():
        @pl.loop(0, count // piece)
        def _(k):
            at = pl.ds(pl.multiple_of(k * piece, piece), piece)
            out_ref[:, at] = acc[:, at] + acc_t[at, :].T


def local_terms(x, dissimilarity, per_root):
    dims, count = x.shape
    height, half = dissimilarity.shape
    tile_count = height // (2 * half)
    bf16, f32 = jnp.bfloat16, jnp.float32
    whole = pl.BlockSpec(memory_space=pltpu.VMEM)
    return pl.pallas_call(
        functools.partial(terms_kernel, per_root, tile_count),
        grid=(height // STEP_ROWS,),
        out_shape=jax.ShapeDtypeStruct((dims, count), f32),
        in_specs=[whole, pl.BlockSpec((STEP_ROWS, half), lambda i: (i, 0))],
        out_specs=whole,
        scratch_shapes=[
            pltpu.VMEM((count, 4 * dims), bf16),
            pltpu.VMEM((count, 4 * dims), bf16),
            pltpu.VMEM((4 * dims, count), bf16),
            pltpu.VMEM((2 * dims + 16, count), bf16),
            pltpu.VMEM((count, 1), f32),
            pltpu.VMEM((8, count), f32),
            pltpu.VMEM((count, dims), f32),
            pltpu.VMEM((count, dims), f32),
            pltpu.VMEM((dims, count), f32),
        ],
        compiler_params=pltpu.CompilerParams(vmem_limit_bytes=56 * 1024 * 1024),
    )(x, dissimilarity)


def exchange_kernel(scatter, gather, n_row, n_col, slow, fast, width, inverse, *refs):
    refs = list(refs)
    in_ref, out_ref = refs[0], refs[1]
    if scatter:
        (work, own, core_buf, sum_buf, row_buf, x_buf, up_buf, down_buf,
         core_s, core_r, row_s, row_r, x_s, x_r, up_s, up_r, down_s, down_r) = refs[2:20]
        refs = refs[20:]
    else:
        refs = refs[2:]
    if gather:
        gup_s, gup_r, gdown_s, gdown_r, gx_s, gx_r, grow_s, gcore_s, gcol_r = refs
    per_root = n_col // n_row
    per_block = n_col // per_root
    height = n_col * width
    row_pos = lax.axis_index("row")
    col_pos = lax.axis_index("col")
    z, x = col_pos // fast, col_pos % fast
    which = col_pos % per_root
    root = col_pos // per_root
    at_root = row_pos == root
    same_core = row_pos % 2 == root % 2
    relays = same_core & (row_pos != root)
    groups = n_row // 2
    group, core = row_pos // 2, row_pos % 2
    has_up, has_down = z < slow - 1, z > 0
    above, below = {"col": (z + 1) * fast + x}, {"col": (z - 1) * fast + x}
    core_peer = {"row": group * 2 + 1 - core}
    sent = []

    def beside(e):
        return {"col": z * fast + (x + e) % fast}

    def when(pred, body):
        if pred is True:
            body()
        else:
            pl.when(pred)(body)

    def send(pred, make):
        when(pred, lambda: make().start())
        sent.append((pred, make))

    def remote(src, dst, send_sem, recv_sem, peer):
        return pltpu.make_async_remote_copy(
            src_ref=src, dst_ref=dst, send_sem=send_sem, recv_sem=recv_sem,
            device_id=peer, device_id_type=pl.DeviceIdType.MESH,
        )

    def arrived(dst, recv_sem):
        remote(dst, dst, recv_sem, recv_sem, core_peer).wait_recv()

    def chunk(zz, xx):
        return pl.ds(pl.multiple_of((zz * fast + xx) * width, width), width)

    def column(kk):
        return pl.ds(pl.multiple_of(height + kk * width, width), width)

    barrier = pltpu.get_barrier_semaphore()

    def greet(peer):
        pl.semaphore_signal(barrier, inc=1, device_id=peer, device_id_type=pl.DeviceIdType.MESH)

    when(has_up, lambda: greet(above))
    when(has_down, lambda: greet(below))
    for e in range(1, fast):
        greet(beside(e))
    for g in range(1, groups):
        greet({"row": (group + g) % groups * 2 + core})
    greet(core_peer)
    neighbours = jnp.where(has_up, 1, 0) + jnp.where(has_down, 1, 0)
    pl.semaphore_wait(barrier, fast - 1 + groups + neighbours)

    if scatter:
        for kk in range(per_block):
            send(jnp.logical_not(same_core), lambda kk=kk: remote(
                in_ref.at[:, column(kk)], core_buf.at[kk], core_s.at[kk], core_r.at[kk], core_peer))
        work[...] = in_ref[:, :height]
        shift = (which + 1) * per_block // fast % slow
        for k in range(slow):
            zz = (k + shift) % slow

            def settle(zz=zz):
                for xx in range(fast):
                    kk = zz * fast + xx - which * per_block
                    arrived(core_buf.at[kk], core_r.at[kk])
                    total = work[:, chunk(zz, xx)] + in_ref[:, column(kk)] + core_buf[kk]
                    for g in range(1, groups):
                        other = (group + g) % groups
                        arrived(row_buf.at[other, kk], row_r.at[other, kk])
                        total += row_buf[other, kk]
                    work[:, chunk(zz, xx)] = total

            when(at_root & (zz * fast // per_block == which), settle)
            for e in range(1, fast):
                send(True, lambda zz=zz, e=e: remote(
                    work.at[:, chunk(zz, (x + e) % fast)], x_buf.at[e - 1, zz],
                    x_s.at[e - 1, zz], x_r.at[e - 1, zz], beside(e)))
        for kk in range(per_block):
            def relay_sum(kk=kk):
                arrived(core_buf.at[kk], core_r.at[kk])
                sum_buf[kk] = in_ref[:, column(kk)] + core_buf[kk]
            when(relays, relay_sum)
            send(relays, lambda kk=kk: remote(
                sum_buf.at[kk], row_buf.at[group, kk], row_s.at[kk], row_r.at[group, kk], {"row": root}))

        def across(zz):
            total = work[:, chunk(zz, x)]
            for e in range(1, fast):
                arrived(x_buf.at[e - 1, zz], x_r.at[e - 1, zz])
                total += x_buf[e - 1, zz]
            return total

        def pass_on(zz, has_behind, buf, recv):
            total = across(zz)
            work[:, chunk(zz, x)] = total

            @pl.when(has_behind)
            def _():
                arrived(buf.at[zz], recv.at[zz])
                work[:, chunk(zz, x)] += buf[zz]

        for d in range(slow - 1, 0, -1):
            when(z + d < slow, lambda d=d: pass_on(z + d, has_down, up_buf, up_r))
            send(z + d < slow, lambda d=d: remote(
                work.at[:, chunk(z + d, x)], up_buf.at[z + d], up_s.at[z + d], up_r.at[z + d], above))
            when(z - d >= 0, lambda d=d: pass_on(z - d, has_up, down_buf, down_r))
            send(z - d >= 0, lambda d=d: remote(
                work.at[:, chunk(z - d, x)], down_buf.at[z - d], down_s.at[z - d], down_r.at[z - d], below))
        own[...] = across(z)

        @pl.when(has_down)
        def _():
            arrived(up_buf.at[z], up_r.at[z])
            own[...] += up_buf[z]

        @pl.when(has_up)
        def _():
            arrived(down_buf.at[z], down_r.at[z])
            own[...] += down_buf[z]

        mine = own[...] * inverse
    else:
        mine = in_ref[...]

    if gather:
        out_ref[:, chunk(z, x)] = mine

        def hand_on(zz, pred, upward, downward):
            there = out_ref.at[:, chunk(zz, x)]
            if upward is not None:
                send(upward, lambda: remote(there, there, gup_s.at[zz], gup_r.at[zz], above))
            if downward is not None:
                send(downward, lambda: remote(there, there, gdown_s.at[zz], gdown_r.at[zz], below))
            for e in range(1, fast):
                send(pred, lambda e=e: remote(
                    there, there, gx_s.at[e - 1, zz], gx_r.at[e - 1, zz], beside(e)))

        def to_column(zz, xx, pred):
            kk = zz * fast + xx - which * per_block
            wanted = at_root & ((zz * fast + xx) // per_block == which)
            if pred is not True:
                wanted = wanted & pred

            def place():
                out_ref[:, column(kk)] = out_ref[:, chunk(zz, xx)]

            for g in range(1, groups):
                send(wanted, lambda g=g: remote(
                    out_ref.at[:, chunk(zz, xx)], out_ref.at[:, column(kk)],
                    grow_s.at[g - 1, kk], gcol_r.at[kk], {"row": (group + g) % groups * 2 + core}))
            send(wanted, lambda: remote(
                out_ref.at[:, chunk(zz, xx)], out_ref.at[:, column(kk)],
                gcore_s.at[kk], gcol_r.at[kk], core_peer))
            when(wanted, place)

        def from_beside(zz, pred):
            for e in range(1, fast):
                xx = (x + fast - e) % fast
                when(pred, lambda: arrived(out_ref.at[:, chunk(zz, xx)], gx_r.at[e - 1, zz]))
                to_column(zz, xx, pred)

        hand_on(z, True, has_up, has_down)
        to_column(z, x, True)
        for d in range(1, slow):
            low, high = z - d, z + d
            when(low >= 0, lambda: arrived(out_ref.at[:, chunk(low, x)], gup_r.at[low]))
            hand_on(low, low >= 0, (low >= 0) & has_up, None)
            to_column(low, x, low >= 0)
            when(high < slow, lambda: arrived(out_ref.at[:, chunk(high, x)], gdown_r.at[high]))
            hand_on(high, high < slow, None, (high < slow) & has_down)
            to_column(high, x, high < slow)
            if d == 1:
                from_beside(z, True)
            else:
                from_beside(low + 1, low + 1 >= 0)
                from_beside(high - 1, high - 1 < slow)
        from_beside(z - slow + 1, z - slow + 1 >= 0)
        from_beside(z + slow - 1, z + slow - 1 < slow)
        for kk in range(per_block):
            when(jnp.logical_not(at_root), lambda: arrived(out_ref.at[:, column(kk)], gcol_r.at[kk]))
            send(relays, lambda kk=kk: remote(
                out_ref.at[:, column(kk)], out_ref.at[:, column(kk)],
                gcore_s.at[kk], gcol_r.at[kk], core_peer))
    else:
        out_ref[...] = mine
    for pred, make in sent:
        when(pred, lambda: make().wait_send())


def exchange(value, scatter, gather, n_row, n_col, width, inverse, collective_id):
    fast = 1
    while fast * fast * 4 <= n_col:
        fast *= 2
    slow = n_col // fast
    per_block = n_row
    dims = value.shape[0]
    f32 = jnp.float32
    dma = pltpu.SemaphoreType.DMA
    total = (n_col + per_block) * width
    scratch = []
    if scatter:
        piece = (dims, width)
        groups = n_row // 2
        scratch += [
            pltpu.VMEM((dims, n_col * width), f32),
            pltpu.VMEM(piece, f32),
            pltpu.VMEM((per_block,) + piece, f32),
            pltpu.VMEM((per_block,) + piece, f32),
            pltpu.VMEM((groups, per_block) + piece, f32),
            pltpu.VMEM((fast - 1, slow) + piece, f32),
            pltpu.VMEM((slow,) + piece, f32),
            pltpu.VMEM((slow,) + piece, f32),
            dma((per_block,)), dma((per_block,)), dma((per_block,)), dma((groups, per_block)),
            dma((fast - 1, slow)), dma((fast - 1, slow)),
            dma((slow,)), dma((slow,)), dma((slow,)), dma((slow,)),
        ]
    if gather:
        scratch += [
            dma((slow,)), dma((slow,)), dma((slow,)), dma((slow,)),
            dma((fast - 1, slow)), dma((fast - 1, slow)),
            dma((max(n_row // 2 - 1, 1), per_block)), dma((per_block,)), dma((per_block,)),
        ]
    whole = pl.BlockSpec(memory_space=pltpu.VMEM)
    return pl.pallas_call(
        functools.partial(
            exchange_kernel, scatter, gather, n_row, n_col, slow, fast, width, inverse
        ),
        out_shape=jax.ShapeDtypeStruct((dims, total if gather else width), f32),
        in_specs=[whole],
        out_specs=whole,
        scratch_shapes=scratch,
        compiler_params=pltpu.CompilerParams(
            collective_id=collective_id, has_side_effects=True, vmem_limit_bytes=48 * 1024 * 1024
        ),
    )(value)


def local(coords, dissimilarity):
    n_row, n_col = lax.axis_size("row"), lax.axis_size("col")
    width = coords.shape[1]
    inverse = 1.0 / (width * n_row * n_col)
    trade = functools.partial(exchange, n_row=n_row, n_col=n_col, width=width, inverse=inverse)
    both = trade(coords, False, True, collective_id=0)
    for iteration in range(ITERS):
        parts = local_terms(both, dissimilarity, n_col // n_row)
        last = iteration == ITERS - 1
        both = trade(parts, True, not last, collective_id=1 + iteration)
    return both


def solution(mesh):
    in_specs = (P(None, ("row", "col")), P("row", "col"))
    out_specs = P(None, ("row", "col"))
    return jax.shard_map(local, mesh=mesh, in_specs=in_specs, out_specs=out_specs, check_vma=False)
```

```python
import functools

import jax
import jax.numpy as jnp
from jax import lax
from jax.experimental import pallas as pl
from jax.experimental.pallas import tpu as pltpu
from jax.sharding import PartitionSpec as P

ITERS = 2
STEP_ROWS = 512


def terms_kernel(
    per_root, tile_count, x_ref, delta_ref, out_ref,
    lead_ref, trail_ref, push_ref, norm_col, norm_row,
):
    half = delta_ref.shape[1]
    block = 2 * half
    dims, count = x_ref.shape
    rows = delta_ref.shape[0]
    cols_at = tile_count * block
    step = pl.program_id(0)
    row_pos = lax.axis_index("row")
    col_pos = lax.axis_index("col")
    bf16, f32 = jnp.bfloat16, jnp.float32
    piece = 512

    @pl.when(step == 0)
    def _prepare():
        @pl.loop(0, count // piece)
        def _(k):
            at = pl.ds(pl.multiple_of(k * piece, piece), piece)
            x = x_ref[:, at]
            hi = x.astype(bf16).astype(f32)
            lo = (x - hi).astype(bf16).astype(f32)
            kept = hi + lo
            norms = jnp.sum(kept * kept, axis=0, keepdims=True)
            norm_row[:, at] = jnp.broadcast_to(norms, (8, piece))
            norm_col[at, :] = jnp.broadcast_to(norms + 1.0, (128, piece)).T
            trail_ref[:, at] = jnp.concatenate([hi, hi, lo, lo], axis=0).astype(bf16) * -2.0
            stack = jnp.concatenate([hi, lo], axis=0).astype(bf16)
            push_ref[:, at] = jnp.concatenate([stack, jnp.ones((16, piece), bf16)], axis=0)
            flipped = stack.T
            lead_ref[at, :] = jnp.concatenate([flipped, flipped], axis=1)
            out_ref[:, at] = jnp.zeros((dims, piece), f32)

    def spacing(lead, trail):
        gram = jnp.dot(lead_ref[lead, :], trail_ref[:, trail], preferred_element_type=f32)
        wide = jnp.concatenate([norm_col[lead, :]] * (half // 128), axis=1)
        return gram + (wide + norm_row[0:1, trail])

    def add_terms(lead, trail, ratios):
        ratios = ratios.astype(bf16)
        pulled = lax.dot_general(
            push_ref[:, trail], ratios, (((1,), (1,)), ((), ())), preferred_element_type=f32
        )
        pushed = jnp.dot(push_ref[:, lead], ratios, preferred_element_type=f32)
        for at, moved in ((lead, pulled), (trail, pushed)):
            out_ref[:, at] += x_ref[:, at] * moved[2 * dims:2 * dims + 1, :] - (
                moved[:dims, :] + moved[dims:2 * dims, :]
            )

    steps_per_tile = block // rows
    slot = step // steps_per_tile
    first = (step % steps_per_tile) * rows
    row_index = row_pos * per_root + slot
    upper = (row_index == col_pos) & (first < half)
    slot_at = slot * block

    @pl.when(jnp.logical_not(upper))
    def _plain():
        lead_at = jnp.where(row_index > col_pos, cols_at, slot_at) + first
        trail_at = jnp.where(
            row_index < col_pos, cols_at,
            jnp.where(row_index > col_pos, slot_at + half, slot_at),
        )
        lead = pl.ds(pl.multiple_of(lead_at, rows), rows)
        trail = pl.ds(pl.multiple_of(trail_at, half), half)
        add_terms(lead, trail, delta_ref[...] * lax.rsqrt(spacing(lead, trail)))

    @pl.when(upper)
    def _split():
        early_lead = pl.ds(pl.multiple_of(slot_at + first, rows), rows)
        early_trail = pl.ds(pl.multiple_of(slot_at, half), half)
        late_lead = pl.ds(pl.multiple_of(slot_at + half + first, rows), rows)
        late_trail = pl.ds(pl.multiple_of(slot_at + half, half), half)
        row_iota = first + lax.broadcasted_iota(jnp.int32, (rows, half), 0)
        col_iota = lax.broadcasted_iota(jnp.int32, (rows, half), 1)
        early = jnp.where(
            col_iota > row_iota,
            delta_ref[...] * lax.rsqrt(spacing(early_lead, early_trail)), 0.0,
        )
        add_terms(early_lead, early_trail, early)
        late = jnp.where(
            col_iota < row_iota,
            delta_ref[...] * lax.rsqrt(spacing(late_lead, late_trail)), 0.0,
        )
        add_terms(late_lead, late_trail, late)


def local_terms(x, dissimilarity, per_root):
    dims, count = x.shape
    height, half = dissimilarity.shape
    tile_count = height // (2 * half)
    bf16, f32 = jnp.bfloat16, jnp.float32
    whole = pl.BlockSpec(memory_space=pltpu.VMEM)
    return pl.pallas_call(
        functools.partial(terms_kernel, per_root, tile_count),
        grid=(height // STEP_ROWS,),
        out_shape=jax.ShapeDtypeStruct((dims, count), f32),
        in_specs=[whole, pl.BlockSpec((STEP_ROWS, half), lambda i: (i, 0))],
        out_specs=whole,
        scratch_shapes=[
            pltpu.VMEM((count, 4 * dims), bf16),
            pltpu.VMEM((4 * dims, count), bf16),
            pltpu.VMEM((2 * dims + 16, count), bf16),
            pltpu.VMEM((count, 128), f32),
            pltpu.VMEM((8, count), f32),
        ],
        compiler_params=pltpu.CompilerParams(vmem_limit_bytes=56 * 1024 * 1024),
    )(x, dissimilarity)


def exchange_kernel(scatter, gather, n_row, n_col, slow, fast, width, inverse, *refs):
    refs = list(refs)
    in_ref, out_ref = refs[0], refs[1]
    if scatter:
        (work, own, core_buf, sum_buf, row_buf, x_buf, up_buf, down_buf,
         late_buf, late_s, late_r, core_s, core_r, row_s, row_r, x_s, x_r, up_s, up_r, down_s, down_r) = refs[2:23]
        refs = refs[23:]
    else:
        refs = refs[2:]
    if gather:
        gup_s, gup_r, gdown_s, gdown_r, gx_s, gx_r, grow_s, gcore_s, gcol_r = refs
    per_root = n_col // n_row
    per_block = n_col // per_root
    height = n_col * width
    row_pos = lax.axis_index("row")
    col_pos = lax.axis_index("col")
    z, x = col_pos // fast, col_pos % fast
    which = col_pos % per_root
    root = col_pos // per_root
    at_root = row_pos == root
    same_core = row_pos % 2 == root % 2
    relays = same_core & (row_pos != root)
    groups = n_row // 2
    group, core = row_pos // 2, row_pos % 2
    has_up, has_down = z < slow - 1, z > 0
    above, below = {"col": (z + 1) * fast + x}, {"col": (z - 1) * fast + x}
    core_peer = {"row": group * 2 + 1 - core}
    sent = []

    def beside(e):
        return {"col": z * fast + (x + e) % fast}

    def when(pred, body):
        if pred is True:
            body()
        else:
            pl.when(pred)(body)

    def send(pred, make):
        when(pred, lambda: make().start())
        sent.append((pred, make))

    def remote(src, dst, send_sem, recv_sem, peer):
        return pltpu.make_async_remote_copy(
            src_ref=src, dst_ref=dst, send_sem=send_sem, recv_sem=recv_sem,
            device_id=peer, device_id_type=pl.DeviceIdType.MESH,
        )

    def arrived(dst, recv_sem):
        remote(dst, dst, recv_sem, recv_sem, core_peer).wait_recv()

    def chunk(zz, xx):
        return pl.ds(pl.multiple_of((zz * fast + xx) * width, width), width)

    def column(kk):
        return pl.ds(pl.multiple_of(height + kk * width, width), width)

    barrier = pltpu.get_barrier_semaphore()

    def greet(peer):
        pl.semaphore_signal(barrier, inc=1, device_id=peer, device_id_type=pl.DeviceIdType.MESH)

    when(has_up, lambda: greet(above))
    when(has_down, lambda: greet(below))
    for e in range(1, fast):
        greet(beside(e))
    for g in range(1, groups):
        greet({"row": (group + g) % groups * 2 + core})
    greet(core_peer)
    neighbours = jnp.where(has_up, 1, 0) + jnp.where(has_down, 1, 0)
    my_root = row_pos * per_root + col_pos // per_block
    if scatter:
        when(my_root != col_pos, lambda: greet({"col": my_root}))
        neighbours += jnp.where(my_root != col_pos, 1, 0)
        for kk in range(per_block):
            owned = at_root & (which * per_block + kk != col_pos)
            when(owned, lambda: greet({"col": which * per_block + kk}))
            neighbours += jnp.where(owned, 1, 0)
    pl.semaphore_wait(barrier, fast - 1 + groups + neighbours)

    if scatter:
        for kk in range(per_block):
            send(jnp.logical_not(same_core), lambda kk=kk: remote(
                in_ref.at[:, column(kk)], core_buf.at[kk], core_s.at[kk], core_r.at[kk], core_peer))
        order = [z + d for d in range(slow - 1, 0, -1)] + [z - d for d in range(slow - 1, 0, -1)]
        order = [order[i + h * (slow - 1)] for i in range(slow - 1) for h in range(2)] + [z]
        for zz in order:
            for e in range(1, fast):
                send((zz >= 0) & (zz < slow), lambda zz=zz, e=e: remote(
                    in_ref.at[:, chunk(zz, (x + e) % fast)], x_buf.at[e - 1, zz],
                    x_s.at[e - 1, zz], x_r.at[e - 1, zz], beside(e)))
        for kk in range(per_block):
            def relay_sum(kk=kk):
                arrived(core_buf.at[kk], core_r.at[kk])
                sum_buf[kk] = in_ref[:, column(kk)] + core_buf[kk]
            when(relays, relay_sum)
            send(relays, lambda kk=kk: remote(
                sum_buf.at[kk], row_buf.at[group, kk], row_s.at[kk], row_r.at[group, kk], {"row": root}))

        def settle(kk):
            arrived(core_buf.at[kk], core_r.at[kk])
            total = in_ref[:, column(kk)] + core_buf[kk]
            for g in range(1, groups):
                other = (group + g) % groups
                arrived(row_buf.at[other, kk], row_r.at[other, kk])
                total += row_buf[other, kk]
            sum_buf[kk] = total

        def across(zz):
            total = in_ref[:, chunk(zz, x)]
            for e in range(1, fast):
                arrived(x_buf.at[e - 1, zz], x_r.at[e - 1, zz])
                total += x_buf[e - 1, zz]
            return total

        def pass_on(zz, has_behind, buf, recv):
            total = across(zz)
            work[:, chunk(zz, x)] = total

            @pl.when(has_behind)
            def _():
                arrived(buf.at[zz], recv.at[zz])
                work[:, chunk(zz, x)] += buf[zz]

        for d in range(slow - 1, 0, -1):
            when(z + d < slow, lambda d=d: pass_on(z + d, has_down, up_buf, up_r))
            send(z + d < slow, lambda d=d: remote(
                work.at[:, chunk(z + d, x)], up_buf.at[z + d], up_s.at[z + d], up_r.at[z + d], above))
            when(z - d >= 0, lambda d=d: pass_on(z - d, has_up, down_buf, down_r))
            send(z - d >= 0, lambda d=d: remote(
                work.at[:, chunk(z - d, x)], down_buf.at[z - d], down_s.at[z - d], down_r.at[z - d], below))
            for kk in range(per_block):
                if kk * (slow - 1) // per_block == slow - 1 - d:
                    when(at_root, lambda: settle(kk))
                    send(at_root & (which * per_block + kk != col_pos), lambda kk=kk: remote(
                        sum_buf.at[kk], late_buf, late_s.at[kk], late_r,
                        {"col": which * per_block + kk}))
        own[...] = across(z)

        @pl.when(has_down)
        def _():
            arrived(up_buf.at[z], up_r.at[z])
            own[...] += up_buf[z]

        @pl.when(has_up)
        def _():
            arrived(down_buf.at[z], down_r.at[z])
            own[...] += down_buf[z]

        @pl.when(my_root != col_pos)
        def _():
            arrived(late_buf, late_r)
            own[...] += late_buf[...]

        @pl.when(my_root == col_pos)
        def _():
            own[...] += sum_buf[col_pos % per_block]

        mine = own[...] * inverse
    else:
        mine = in_ref[...]

    if gather:
        out_ref[:, chunk(z, x)] = mine

        def hand_on(zz, pred, upward, downward):
            there = out_ref.at[:, chunk(zz, x)]
            if upward is not None:
                send(upward, lambda: remote(there, there, gup_s.at[zz], gup_r.at[zz], above))
            if downward is not None:
                send(downward, lambda: remote(there, there, gdown_s.at[zz], gdown_r.at[zz], below))
            for e in range(1, fast):
                send(pred, lambda e=e: remote(
                    there, there, gx_s.at[e - 1, zz], gx_r.at[e - 1, zz], beside(e)))

        def to_column(zz, xx, pred):
            kk = zz * fast + xx - which * per_block
            wanted = at_root & ((zz * fast + xx) // per_block == which)
            if pred is not True:
                wanted = wanted & pred

            def place():
                out_ref[:, column(kk)] = out_ref[:, chunk(zz, xx)]

            for g in range(1, groups):
                send(wanted, lambda g=g: remote(
                    out_ref.at[:, chunk(zz, xx)], out_ref.at[:, column(kk)],
                    grow_s.at[g - 1, kk], gcol_r.at[kk], {"row": (group + g) % groups * 2 + core}))
            send(wanted, lambda: remote(
                out_ref.at[:, chunk(zz, xx)], out_ref.at[:, column(kk)],
                gcore_s.at[kk], gcol_r.at[kk], core_peer))
            when(wanted, place)

        def from_beside(zz, pred):
            for e in range(1, fast):
                xx = (x + fast - e) % fast
                when(pred, lambda: arrived(out_ref.at[:, chunk(zz, xx)], gx_r.at[e - 1, zz]))
                to_column(zz, xx, pred)

        hand_on(z, True, has_up, has_down)
        to_column(z, x, True)
        for d in range(1, slow):
            low, high = z - d, z + d
            when(low >= 0, lambda: arrived(out_ref.at[:, chunk(low, x)], gup_r.at[low]))
            hand_on(low, low >= 0, (low >= 0) & has_up, None)
            to_column(low, x, low >= 0)
            when(high < slow, lambda: arrived(out_ref.at[:, chunk(high, x)], gdown_r.at[high]))
            hand_on(high, high < slow, None, (high < slow) & has_down)
            to_column(high, x, high < slow)
            if d == 1:
                from_beside(z, True)
            else:
                from_beside(low + 1, low + 1 >= 0)
                from_beside(high - 1, high - 1 < slow)
        from_beside(z - slow + 1, z - slow + 1 >= 0)
        from_beside(z + slow - 1, z + slow - 1 < slow)
        for kk in range(per_block):
            when(jnp.logical_not(at_root), lambda: arrived(out_ref.at[:, column(kk)], gcol_r.at[kk]))
            send(relays, lambda kk=kk: remote(
                out_ref.at[:, column(kk)], out_ref.at[:, column(kk)],
                gcore_s.at[kk], gcol_r.at[kk], core_peer))
    else:
        out_ref[...] = mine
    for pred, make in sent:
        when(pred, lambda: make().wait_send())


def exchange(value, scatter, gather, n_row, n_col, width, inverse, collective_id):
    fast = 1
    while fast * fast * 4 <= n_col:
        fast *= 2
    slow = n_col // fast
    per_block = n_row
    dims = value.shape[0]
    f32 = jnp.float32
    dma = pltpu.SemaphoreType.DMA
    total = (n_col + per_block) * width
    scratch = []
    if scatter:
        piece = (dims, width)
        groups = n_row // 2
        scratch += [
            pltpu.VMEM((dims, n_col * width), f32),
            pltpu.VMEM(piece, f32),
            pltpu.VMEM((per_block,) + piece, f32),
            pltpu.VMEM((per_block,) + piece, f32),
            pltpu.VMEM((groups, per_block) + piece, f32),
            pltpu.VMEM((fast - 1, slow) + piece, f32),
            pltpu.VMEM((slow,) + piece, f32),
            pltpu.VMEM((slow,) + piece, f32),
            pltpu.VMEM(piece, f32), dma((per_block,)), dma,
            dma((per_block,)), dma((per_block,)), dma((per_block,)), dma((groups, per_block)),
            dma((fast - 1, slow)), dma((fast - 1, slow)),
            dma((slow,)), dma((slow,)), dma((slow,)), dma((slow,)),
        ]
    if gather:
        scratch += [
            dma((slow,)), dma((slow,)), dma((slow,)), dma((slow,)),
            dma((fast - 1, slow)), dma((fast - 1, slow)),
            dma((max(n_row // 2 - 1, 1), per_block)), dma((per_block,)), dma((per_block,)),
        ]
    whole = pl.BlockSpec(memory_space=pltpu.VMEM)
    return pl.pallas_call(
        functools.partial(
            exchange_kernel, scatter, gather, n_row, n_col, slow, fast, width, inverse
        ),
        out_shape=jax.ShapeDtypeStruct((dims, total if gather else width), f32),
        in_specs=[whole],
        out_specs=whole,
        scratch_shapes=scratch,
        compiler_params=pltpu.CompilerParams(
            collective_id=collective_id, has_side_effects=True, vmem_limit_bytes=48 * 1024 * 1024
        ),
    )(value)


def local(coords, dissimilarity):
    n_row, n_col = lax.axis_size("row"), lax.axis_size("col")
    width = coords.shape[1]
    inverse = 1.0 / (width * n_row * n_col)
    trade = functools.partial(exchange, n_row=n_row, n_col=n_col, width=width, inverse=inverse)
    both = trade(coords, False, True, collective_id=0)
    for iteration in range(ITERS):
        parts = local_terms(both, dissimilarity, n_col // n_row)
        last = iteration == ITERS - 1
        both = trade(parts, True, not last, collective_id=1 + iteration)
    return both


def solution(mesh):
    in_specs = (P(None, ("row", "col")), P("row", "col"))
    out_specs = P(None, ("row", "col"))
    return jax.shard_map(local, mesh=mesh, in_specs=in_specs, out_specs=out_specs, check_vma=False)
```

```python
import functools

import jax
import jax.numpy as jnp
from jax import lax
from jax.experimental import pallas as pl
from jax.experimental.pallas import tpu as pltpu
from jax.sharding import PartitionSpec as P

ITERS = 2
STEP_ROWS = 512
PARTS = 2


def terms_kernel(
    per_root, tile_count, x_ref, delta_ref, out_ref,
    lead_ref, trail_ref, push_ref, norm_col, norm_row,
):
    half = delta_ref.shape[1]
    block = 2 * half
    dims, count = x_ref.shape
    rows = delta_ref.shape[0]
    cols_at = tile_count * block
    step = pl.program_id(0)
    row_pos = lax.axis_index("row")
    col_pos = lax.axis_index("col")
    bf16, f32 = jnp.bfloat16, jnp.float32
    piece = 1024

    @pl.when(step == 0)
    def _prepare():
        @pl.loop(0, count // piece)
        def _(k):
            at = pl.ds(pl.multiple_of(k * piece, piece), piece)
            x = x_ref[:, at]
            hi = x.astype(bf16).astype(f32)
            lo = (x - hi).astype(bf16).astype(f32)
            kept = hi + lo
            norms = jnp.sum(kept * kept, axis=0, keepdims=True)
            norm_row[:, at] = jnp.broadcast_to(norms, (8, piece))
            norm_col[at, :] = jnp.broadcast_to(norms + 1.0, (128, piece)).T
            trail_ref[:, at] = jnp.concatenate([hi, hi, lo, lo], axis=0).astype(bf16) * -2.0
            stack = jnp.concatenate([hi, lo], axis=0).astype(bf16)
            push_ref[:, at] = jnp.concatenate([stack, jnp.ones((16, piece), bf16)], axis=0)
            flipped = stack.T
            lead_ref[at, :] = jnp.concatenate([flipped, flipped], axis=1)
            out_ref[:, at] = jnp.zeros((dims, piece), f32)

    def spacing(lead, trail):
        gram = jnp.dot(lead_ref[lead, :], trail_ref[:, trail], preferred_element_type=f32)
        wide = jnp.concatenate([norm_col[lead, :]] * (half // 128), axis=1)
        return gram + (wide + norm_row[0:1, trail])

    def add_terms(lead, trail, ratios):
        ratios = ratios.astype(bf16)
        pulled = lax.dot_general(
            push_ref[:, trail], ratios, (((1,), (1,)), ((), ())), preferred_element_type=f32
        )
        pushed = jnp.dot(push_ref[:, lead], ratios, preferred_element_type=f32)
        for at, moved in ((lead, pulled), (trail, pushed)):
            out_ref[:, at] += x_ref[:, at] * moved[2 * dims:2 * dims + 1, :] - (
                moved[:dims, :] + moved[dims:2 * dims, :]
            )

    steps_per_tile = block // rows
    slot = step // steps_per_tile
    first = (step % steps_per_tile) * rows
    row_index = row_pos * per_root + slot
    upper = (row_index == col_pos) & (first < half)
    slot_at = slot * block

    @pl.when(jnp.logical_not(upper))
    def _plain():
        lead_at = jnp.where(row_index > col_pos, cols_at, slot_at) + first
        trail_at = jnp.where(
            row_index < col_pos, cols_at,
            jnp.where(row_index > col_pos, slot_at + half, slot_at),
        )
        lead = pl.ds(pl.multiple_of(lead_at, rows), rows)
        trail = pl.ds(pl.multiple_of(trail_at, half), half)
        add_terms(lead, trail, delta_ref[...] * lax.rsqrt(spacing(lead, trail)))

    @pl.when(upper)
    def _split():
        early_lead = pl.ds(pl.multiple_of(slot_at + first, rows), rows)
        early_trail = pl.ds(pl.multiple_of(slot_at, half), half)
        late_lead = pl.ds(pl.multiple_of(slot_at + half + first, rows), rows)
        late_trail = pl.ds(pl.multiple_of(slot_at + half, half), half)
        row_iota = first + lax.broadcasted_iota(jnp.int32, (rows, half), 0)
        col_iota = lax.broadcasted_iota(jnp.int32, (rows, half), 1)
        early = jnp.where(
            col_iota > row_iota,
            delta_ref[...] * lax.rsqrt(spacing(early_lead, early_trail)), 0.0,
        )
        add_terms(early_lead, early_trail, early)
        late = jnp.where(
            col_iota < row_iota,
            delta_ref[...] * lax.rsqrt(spacing(late_lead, late_trail)), 0.0,
        )
        add_terms(late_lead, late_trail, late)


def local_terms(x, dissimilarity, per_root):
    dims, count = x.shape
    height, half = dissimilarity.shape
    tile_count = height // (2 * half)
    bf16, f32 = jnp.bfloat16, jnp.float32
    whole = pl.BlockSpec(memory_space=pltpu.VMEM)
    return pl.pallas_call(
        functools.partial(terms_kernel, per_root, tile_count),
        grid=(height // STEP_ROWS,),
        out_shape=jax.ShapeDtypeStruct((dims, count), f32),
        in_specs=[whole, pl.BlockSpec((STEP_ROWS, half), lambda i: (i, 0))],
        out_specs=whole,
        scratch_shapes=[
            pltpu.VMEM((count, 4 * dims), bf16),
            pltpu.VMEM((4 * dims, count), bf16),
            pltpu.VMEM((2 * dims + 16, count), bf16),
            pltpu.VMEM((count, 128), f32),
            pltpu.VMEM((8, count), f32),
        ],
        compiler_params=pltpu.CompilerParams(vmem_limit_bytes=56 * 1024 * 1024),
    )(x, dissimilarity)


def exchange_kernel(scatter, gather, n_row, n_col, slow, fast, width, inverse, *refs):
    refs = list(refs)
    in_ref, out_ref = refs[0], refs[1]
    if scatter:
        (work, own, core_buf, sum_buf, row_buf, x_buf, up_buf, down_buf,
         late_buf, late_s, late_r, core_s, core_r, row_s, row_r, x_s, x_r, up_s, up_r, down_s, down_r) = refs[2:23]
        refs = refs[23:]
    else:
        refs = refs[2:]
    if gather:
        gup_s, gup_r, gdown_s, gdown_r, gx_s, gx_r, grow_s, gcore_s, gcol_r = refs
    per_root = n_col // n_row
    per_block = n_col // per_root
    height = n_col * width
    row_pos = lax.axis_index("row")
    col_pos = lax.axis_index("col")
    z, x = col_pos // fast, col_pos % fast
    which = col_pos % per_root
    root = col_pos // per_root
    at_root = row_pos == root
    same_core = row_pos % 2 == root % 2
    relays = same_core & (row_pos != root)
    groups = n_row // 2
    group, core = row_pos // 2, row_pos % 2
    has_up, has_down = z < slow - 1, z > 0
    above, below = {"col": (z + 1) * fast + x}, {"col": (z - 1) * fast + x}
    core_peer = {"row": group * 2 + 1 - core}
    sent = []

    def beside(e):
        return {"col": z * fast + (x + e) % fast}

    def when(pred, body):
        if pred is True:
            body()
        else:
            pl.when(pred)(body)

    def send(pred, make):
        when(pred, lambda: make().start())
        sent.append((pred, make))

    def remote(src, dst, send_sem, recv_sem, peer):
        return pltpu.make_async_remote_copy(
            src_ref=src, dst_ref=dst, send_sem=send_sem, recv_sem=recv_sem,
            device_id=peer, device_id_type=pl.DeviceIdType.MESH,
        )

    def arrived(dst, recv_sem):
        remote(dst, dst, recv_sem, recv_sem, core_peer).wait_recv()

    def chunk(zz, xx):
        return pl.ds(pl.multiple_of((zz * fast + xx) * width, width), width)

    def part(h):
        size = out_ref.shape[0] // PARTS
        return pl.ds(h * size, size)

    def column(kk):
        return pl.ds(pl.multiple_of(height + kk * width, width), width)

    barrier = pltpu.get_barrier_semaphore()

    def greet(peer):
        pl.semaphore_signal(barrier, inc=1, device_id=peer, device_id_type=pl.DeviceIdType.MESH)

    when(has_up, lambda: greet(above))
    when(has_down, lambda: greet(below))
    for e in range(1, fast):
        greet(beside(e))
    for g in range(1, groups):
        greet({"row": (group + g) % groups * 2 + core})
    greet(core_peer)
    neighbours = jnp.where(has_up, 1, 0) + jnp.where(has_down, 1, 0)
    my_root = row_pos * per_root + col_pos // per_block
    if scatter:
        when(my_root != col_pos, lambda: greet({"col": my_root}))
        neighbours += jnp.where(my_root != col_pos, 1, 0)
        for kk in range(per_block):
            owned = at_root & (which * per_block + kk != col_pos)
            when(owned, lambda: greet({"col": which * per_block + kk}))
            neighbours += jnp.where(owned, 1, 0)
    pl.semaphore_wait(barrier, fast - 1 + groups + neighbours)

    if scatter:
        for kk in range(per_block):
            send(jnp.logical_not(same_core), lambda kk=kk: remote(
                in_ref.at[:, column(kk)], core_buf.at[kk], core_s.at[kk], core_r.at[kk], core_peer))
        order = [z + d for d in range(slow - 1, 0, -1)] + [z - d for d in range(slow - 1, 0, -1)]
        order = [order[i + h * (slow - 1)] for i in range(slow - 1) for h in range(2)] + [z]
        for zz in order:
            for e in range(1, fast):
                for h in range(PARTS):
                    send((zz >= 0) & (zz < slow), lambda zz=zz, e=e, h=h: remote(
                        in_ref.at[part(h), chunk(zz, (x + e) % fast)], x_buf.at[e - 1, zz, part(h)],
                        x_s.at[h, e - 1, zz], x_r.at[h, e - 1, zz], beside(e)))
        for kk in range(per_block):
            def relay_sum(kk=kk):
                arrived(core_buf.at[kk], core_r.at[kk])
                sum_buf[kk] = in_ref[:, column(kk)] + core_buf[kk]
            when(relays, relay_sum)
            send(relays, lambda kk=kk: remote(
                sum_buf.at[kk], row_buf.at[group, kk], row_s.at[kk], row_r.at[group, kk], {"row": root}))

        def settle(kk):
            arrived(core_buf.at[kk], core_r.at[kk])
            total = in_ref[:, column(kk)] + core_buf[kk]
            for g in range(1, groups):
                other = (group + g) % groups
                arrived(row_buf.at[other, kk], row_r.at[other, kk])
                total += row_buf[other, kk]
            sum_buf[kk] = total

        def across(h, zz):
            total = in_ref[part(h), chunk(zz, x)]
            for e in range(1, fast):
                arrived(x_buf.at[e - 1, zz, part(h)], x_r.at[h, e - 1, zz])
                total += x_buf[e - 1, zz, part(h)]
            return total

        def pass_on(h, zz, has_behind, buf, recv):
            work[part(h), chunk(zz, x)] = across(h, zz)

            @pl.when(has_behind)
            def _():
                arrived(buf.at[zz, part(h)], recv.at[h, zz])
                work[part(h), chunk(zz, x)] += buf[zz, part(h)]

        for d in range(slow - 1, 0, -1):
            for h in range(PARTS):
                when(z + d < slow, lambda: pass_on(h, z + d, has_down, up_buf, up_r))
                send(z + d < slow, lambda d=d, h=h: remote(
                    work.at[part(h), chunk(z + d, x)], up_buf.at[z + d, part(h)],
                    up_s.at[h, z + d], up_r.at[h, z + d], above))
                when(z - d >= 0, lambda: pass_on(h, z - d, has_up, down_buf, down_r))
                send(z - d >= 0, lambda d=d, h=h: remote(
                    work.at[part(h), chunk(z - d, x)], down_buf.at[z - d, part(h)],
                    down_s.at[h, z - d], down_r.at[h, z - d], below))
            for kk in range(per_block):
                if kk * (slow - 1) // per_block == slow - 1 - d:
                    when(at_root, lambda: settle(kk))
                    send(at_root & (which * per_block + kk != col_pos), lambda kk=kk: remote(
                        sum_buf.at[kk], late_buf, late_s.at[kk], late_r,
                        {"col": which * per_block + kk}))
        def close(h, buf, recv):
            arrived(buf.at[z, part(h)], recv.at[h, z])
            own[part(h), :] += buf[z, part(h)]

        for h in range(PARTS):
            own[part(h), :] = across(h, z)
            when(has_down, lambda: close(h, up_buf, up_r))
            when(has_up, lambda: close(h, down_buf, down_r))

        @pl.when(my_root != col_pos)
        def _():
            arrived(late_buf, late_r)
            own[...] += late_buf[...]

        @pl.when(my_root == col_pos)
        def _():
            own[...] += sum_buf[col_pos % per_block]

        mine = own[...] * inverse
    else:
        mine = in_ref[...]

    if gather:
        out_ref[:, chunk(z, x)] = mine

        def hand_on(h, zz, pred, upward, downward):
            there = out_ref.at[part(h), chunk(zz, x)]
            if upward is not None:
                send(upward, lambda: remote(there, there, gup_s.at[h, zz], gup_r.at[h, zz], above))
            if downward is not None:
                send(downward, lambda: remote(there, there, gdown_s.at[h, zz], gdown_r.at[h, zz], below))
            for e in range(1, fast):
                send(pred, lambda e=e: remote(
                    there, there, gx_s.at[h, e - 1, zz], gx_r.at[h, e - 1, zz], beside(e)))

        def to_column(h, zz, xx, pred):
            kk = zz * fast + xx - which * per_block
            wanted = at_root & ((zz * fast + xx) // per_block == which)
            if pred is not True:
                wanted = wanted & pred

            def place():
                out_ref[part(h), column(kk)] = out_ref[part(h), chunk(zz, xx)]

            for g in range(1, groups):
                send(wanted, lambda g=g: remote(
                    out_ref.at[part(h), chunk(zz, xx)], out_ref.at[part(h), column(kk)],
                    grow_s.at[h, g - 1, kk], gcol_r.at[h, kk], {"row": (group + g) % groups * 2 + core}))
            send(wanted, lambda: remote(
                out_ref.at[part(h), chunk(zz, xx)], out_ref.at[part(h), column(kk)],
                gcore_s.at[h, kk], gcol_r.at[h, kk], core_peer))
            when(wanted, place)

        def from_beside(h, zz, pred):
            for e in range(1, fast):
                xx = (x + fast - e) % fast
                when(pred, lambda: arrived(out_ref.at[part(h), chunk(zz, xx)], gx_r.at[h, e - 1, zz]))
                to_column(h, zz, xx, pred)

        for h in range(PARTS):
            hand_on(h, z, True, has_up, has_down)
            to_column(h, z, x, True)
        for d in range(1, slow):
            low, high = z - d, z + d
            for h in range(PARTS):
                when(low >= 0, lambda: arrived(out_ref.at[part(h), chunk(low, x)], gup_r.at[h, low]))
                hand_on(h, low, low >= 0, (low >= 0) & has_up, None)
                to_column(h, low, x, low >= 0)
                when(high < slow, lambda: arrived(out_ref.at[part(h), chunk(high, x)], gdown_r.at[h, high]))
                hand_on(h, high, high < slow, None, (high < slow) & has_down)
                to_column(h, high, x, high < slow)
                if d == 1:
                    from_beside(h, z, True)
                else:
                    from_beside(h, low + 1, low + 1 >= 0)
                    from_beside(h, high - 1, high - 1 < slow)
        for h in range(PARTS):
            from_beside(h, z - slow + 1, z - slow + 1 >= 0)
            from_beside(h, z + slow - 1, z + slow - 1 < slow)
        for kk in range(per_block):
            for h in range(PARTS):
                when(jnp.logical_not(at_root), lambda: arrived(
                    out_ref.at[part(h), column(kk)], gcol_r.at[h, kk]))
                send(relays, lambda kk=kk, h=h: remote(
                    out_ref.at[part(h), column(kk)], out_ref.at[part(h), column(kk)],
                    gcore_s.at[h, kk], gcol_r.at[h, kk], core_peer))
    else:
        out_ref[...] = mine
    for pred, make in sent:
        when(pred, lambda: make().wait_send())


def exchange(value, scatter, gather, n_row, n_col, width, inverse, collective_id):
    fast = 1
    while fast * fast * 4 <= n_col:
        fast *= 2
    slow = n_col // fast
    per_block = n_row
    dims = value.shape[0]
    f32 = jnp.float32
    dma = pltpu.SemaphoreType.DMA
    total = (n_col + per_block) * width
    scratch = []
    if scatter:
        piece = (dims, width)
        groups = n_row // 2
        scratch += [
            pltpu.VMEM((dims, n_col * width), f32),
            pltpu.VMEM(piece, f32),
            pltpu.VMEM((per_block,) + piece, f32),
            pltpu.VMEM((per_block,) + piece, f32),
            pltpu.VMEM((groups, per_block) + piece, f32),
            pltpu.VMEM((fast - 1, slow) + piece, f32),
            pltpu.VMEM((slow,) + piece, f32),
            pltpu.VMEM((slow,) + piece, f32),
            pltpu.VMEM(piece, f32), dma((per_block,)), dma,
            dma((per_block,)), dma((per_block,)), dma((per_block,)), dma((groups, per_block)),
            dma((PARTS, fast - 1, slow)), dma((PARTS, fast - 1, slow)),
            dma((PARTS, slow)), dma((PARTS, slow)), dma((PARTS, slow)), dma((PARTS, slow)),
        ]
    if gather:
        scratch += [
            dma((PARTS, slow)), dma((PARTS, slow)), dma((PARTS, slow)), dma((PARTS, slow)),
            dma((PARTS, fast - 1, slow)), dma((PARTS, fast - 1, slow)),
            dma((PARTS, max(n_row // 2 - 1, 1), per_block)), dma((PARTS, per_block)), dma((PARTS, per_block)),
        ]
    whole = pl.BlockSpec(memory_space=pltpu.VMEM)
    return pl.pallas_call(
        functools.partial(
            exchange_kernel, scatter, gather, n_row, n_col, slow, fast, width, inverse
        ),
        out_shape=jax.ShapeDtypeStruct((dims, total if gather else width), f32),
        in_specs=[whole],
        out_specs=whole,
        scratch_shapes=scratch,
        compiler_params=pltpu.CompilerParams(
            collective_id=collective_id, has_side_effects=True, vmem_limit_bytes=48 * 1024 * 1024
        ),
    )(value)


def local(coords, dissimilarity):
    n_row, n_col = lax.axis_size("row"), lax.axis_size("col")
    width = coords.shape[1]
    inverse = 1.0 / (width * n_row * n_col)
    trade = functools.partial(exchange, n_row=n_row, n_col=n_col, width=width, inverse=inverse)
    both = trade(coords, False, True, collective_id=0)
    for iteration in range(ITERS):
        parts = local_terms(both, dissimilarity, n_col // n_row)
        last = iteration == ITERS - 1
        both = trade(parts, True, not last, collective_id=1 + iteration)
    return both


def solution(mesh):
    in_specs = (P(None, ("row", "col")), P("row", "col"))
    out_specs = P(None, ("row", "col"))
    return jax.shard_map(local, mesh=mesh, in_specs=in_specs, out_specs=out_specs, check_vma=False)
```

```python
import functools

import jax
import jax.numpy as jnp
from jax import lax
from jax.experimental import pallas as pl
from jax.experimental.pallas import tpu as pltpu
from jax.sharding import PartitionSpec as P

ITERS = 2
STEP_ROWS = 512
PARTS = 4


def terms_kernel(
    per_root, tile_count, x_ref, delta_ref, out_ref,
    lead_ref, trail_ref, push_ref, norm_col, norm_row,
):
    half = delta_ref.shape[1]
    block = 2 * half
    dims, count = x_ref.shape
    rows = delta_ref.shape[0]
    cols_at = tile_count * block
    step = pl.program_id(0)
    row_pos = lax.axis_index("row")
    col_pos = lax.axis_index("col")
    bf16, f32 = jnp.bfloat16, jnp.float32
    piece = 1024

    @pl.when(step == 0)
    def _prepare():
        @pl.loop(0, count // piece)
        def _(k):
            at = pl.ds(pl.multiple_of(k * piece, piece), piece)
            x = x_ref[:, at]
            hi = x.astype(bf16).astype(f32)
            lo = (x - hi).astype(bf16).astype(f32)
            kept = hi + lo
            norms = jnp.sum(kept * kept, axis=0, keepdims=True)
            norm_row[:, at] = jnp.broadcast_to(norms, (8, piece))
            norm_col[at, :] = jnp.broadcast_to(norms + 1.0, (128, piece)).T
            trail_ref[:, at] = jnp.concatenate([hi, hi, lo, lo], axis=0).astype(bf16) * -2.0
            stack = jnp.concatenate([hi, lo], axis=0).astype(bf16)
            push_ref[:, at] = jnp.concatenate([stack, jnp.ones((16, piece), bf16)], axis=0)
            flipped = stack.T
            lead_ref[at, :] = jnp.concatenate([flipped, flipped], axis=1)
            out_ref[:, at] = jnp.zeros((dims, piece), f32)

    def spacing(lead, trail):
        gram = jnp.dot(lead_ref[lead, :], trail_ref[:, trail], preferred_element_type=f32)
        wide = jnp.concatenate([norm_col[lead, :]] * (half // 128), axis=1)
        return gram + (wide + norm_row[0:1, trail])

    def add_terms(lead, trail, ratios):
        ratios = ratios.astype(bf16)
        pulled = lax.dot_general(
            push_ref[:, trail], ratios, (((1,), (1,)), ((), ())), preferred_element_type=f32
        )
        pushed = jnp.dot(push_ref[:, lead], ratios, preferred_element_type=f32)
        for at, moved in ((lead, pulled), (trail, pushed)):
            out_ref[:, at] += x_ref[:, at] * moved[2 * dims:2 * dims + 1, :] - (
                moved[:dims, :] + moved[dims:2 * dims, :]
            )

    steps_per_tile = block // rows
    slot = step // steps_per_tile
    first = (step % steps_per_tile) * rows
    row_index = row_pos * per_root + slot
    upper = (row_index == col_pos) & (first < half)
    slot_at = slot * block

    @pl.when(jnp.logical_not(upper))
    def _plain():
        lead_at = jnp.where(row_index > col_pos, cols_at, slot_at) + first
        trail_at = jnp.where(
            row_index < col_pos, cols_at,
            jnp.where(row_index > col_pos, slot_at + half, slot_at),
        )
        lead = pl.ds(pl.multiple_of(lead_at, rows), rows)
        trail = pl.ds(pl.multiple_of(trail_at, half), half)
        add_terms(lead, trail, delta_ref[...] * lax.rsqrt(spacing(lead, trail)))

    @pl.when(upper)
    def _split():
        early_lead = pl.ds(pl.multiple_of(slot_at + first, rows), rows)
        early_trail = pl.ds(pl.multiple_of(slot_at, half), half)
        late_lead = pl.ds(pl.multiple_of(slot_at + half + first, rows), rows)
        late_trail = pl.ds(pl.multiple_of(slot_at + half, half), half)
        row_iota = first + lax.broadcasted_iota(jnp.int32, (rows, half), 0)
        col_iota = lax.broadcasted_iota(jnp.int32, (rows, half), 1)
        early = jnp.where(
            col_iota > row_iota,
            delta_ref[...] * lax.rsqrt(spacing(early_lead, early_trail)), 0.0,
        )
        add_terms(early_lead, early_trail, early)
        late = jnp.where(
            col_iota < row_iota,
            delta_ref[...] * lax.rsqrt(spacing(late_lead, late_trail)), 0.0,
        )
        add_terms(late_lead, late_trail, late)


def local_terms(x, dissimilarity, per_root):
    dims, count = x.shape
    height, half = dissimilarity.shape
    tile_count = height // (2 * half)
    bf16, f32 = jnp.bfloat16, jnp.float32
    whole = pl.BlockSpec(memory_space=pltpu.VMEM)
    return pl.pallas_call(
        functools.partial(terms_kernel, per_root, tile_count),
        grid=(height // STEP_ROWS,),
        out_shape=jax.ShapeDtypeStruct((dims, count), f32),
        in_specs=[whole, pl.BlockSpec((STEP_ROWS, half), lambda i: (i, 0))],
        out_specs=whole,
        scratch_shapes=[
            pltpu.VMEM((count, 4 * dims), bf16),
            pltpu.VMEM((4 * dims, count), bf16),
            pltpu.VMEM((2 * dims + 16, count), bf16),
            pltpu.VMEM((count, 128), f32),
            pltpu.VMEM((8, count), f32),
        ],
        compiler_params=pltpu.CompilerParams(vmem_limit_bytes=56 * 1024 * 1024),
    )(x, dissimilarity)


def exchange_kernel(scatter, gather, n_row, n_col, slow, fast, width, inverse, *refs):
    refs = list(refs)
    in_ref, out_ref = refs[0], refs[1]
    if scatter:
        (work, own, core_buf, sum_buf, row_buf, x_buf, up_buf, down_buf,
         late_buf, late_s, late_r, core_s, core_r, row_s, row_r, x_s, x_r, up_s, up_r, down_s, down_r) = refs[2:23]
        refs = refs[23:]
    else:
        refs = refs[2:]
    if gather:
        gup_s, gup_r, gdown_s, gdown_r, gx_s, gx_r, grow_s, gcore_s, gcol_r = refs
    per_root = n_col // n_row
    per_block = n_col // per_root
    height = n_col * width
    row_pos = lax.axis_index("row")
    col_pos = lax.axis_index("col")
    z, x = col_pos // fast, col_pos % fast
    which = col_pos % per_root
    root = col_pos // per_root
    at_root = row_pos == root
    same_core = row_pos % 2 == root % 2
    relays = same_core & (row_pos != root)
    groups = n_row // 2
    group, core = row_pos // 2, row_pos % 2
    has_up, has_down = z < slow - 1, z > 0
    above, below = {"col": (z + 1) * fast + x}, {"col": (z - 1) * fast + x}
    core_peer = {"row": group * 2 + 1 - core}
    sent = []

    def beside(e):
        return {"col": z * fast + (x + e) % fast}

    def when(pred, body):
        if pred is True:
            body()
        else:
            pl.when(pred)(body)

    def send(pred, make):
        when(pred, lambda: make().start())
        sent.append((pred, make))

    def remote(src, dst, send_sem, recv_sem, peer):
        return pltpu.make_async_remote_copy(
            src_ref=src, dst_ref=dst, send_sem=send_sem, recv_sem=recv_sem,
            device_id=peer, device_id_type=pl.DeviceIdType.MESH,
        )

    def arrived(dst, recv_sem):
        remote(dst, dst, recv_sem, recv_sem, core_peer).wait_recv()

    def chunk(zz, xx):
        return pl.ds(pl.multiple_of((zz * fast + xx) * width, width), width)

    def part(h):
        size = out_ref.shape[0] // PARTS
        return pl.ds(h * size, size)

    def column(kk):
        return pl.ds(pl.multiple_of(height + kk * width, width), width)

    barrier = pltpu.get_barrier_semaphore()

    def greet(peer):
        pl.semaphore_signal(barrier, inc=1, device_id=peer, device_id_type=pl.DeviceIdType.MESH)

    when(has_up, lambda: greet(above))
    when(has_down, lambda: greet(below))
    for e in range(1, fast):
        greet(beside(e))
    for g in range(1, groups):
        greet({"row": (group + g) % groups * 2 + core})
    greet(core_peer)
    neighbours = jnp.where(has_up, 1, 0) + jnp.where(has_down, 1, 0)
    my_root = row_pos * per_root + col_pos // per_block
    if scatter:
        when(my_root != col_pos, lambda: greet({"col": my_root}))
        neighbours += jnp.where(my_root != col_pos, 1, 0)
        for kk in range(per_block):
            owned = at_root & (which * per_block + kk != col_pos)
            when(owned, lambda: greet({"col": which * per_block + kk}))
            neighbours += jnp.where(owned, 1, 0)
    pl.semaphore_wait(barrier, fast - 1 + groups + neighbours)

    if scatter:
        for kk in range(per_block):
            send(jnp.logical_not(same_core), lambda kk=kk: remote(
                in_ref.at[:, column(kk)], core_buf.at[kk], core_s.at[kk], core_r.at[kk], core_peer))
        order = [z + d for d in range(slow - 1, 0, -1)] + [z - d for d in range(slow - 1, 0, -1)]
        order = [order[i + h * (slow - 1)] for i in range(slow - 1) for h in range(2)] + [z]
        for zz in order:
            for e in range(1, fast):
                for h in range(PARTS):
                    send((zz >= 0) & (zz < slow), lambda zz=zz, e=e, h=h: remote(
                        in_ref.at[part(h), chunk(zz, (x + e) % fast)], x_buf.at[e - 1, zz, part(h)],
                        x_s.at[h, e - 1, zz], x_r.at[h, e - 1, zz], beside(e)))
        for kk in range(per_block):
            def relay_sum(kk=kk):
                arrived(core_buf.at[kk], core_r.at[kk])
                sum_buf[kk] = in_ref[:, column(kk)] + core_buf[kk]
            when(relays, relay_sum)
            send(relays, lambda kk=kk: remote(
                sum_buf.at[kk], row_buf.at[group, kk], row_s.at[kk], row_r.at[group, kk], {"row": root}))

        def settle(kk):
            arrived(core_buf.at[kk], core_r.at[kk])
            total = in_ref[:, column(kk)] + core_buf[kk]
            for g in range(1, groups):
                other = (group + g) % groups
                arrived(row_buf.at[other, kk], row_r.at[other, kk])
                total += row_buf[other, kk]
            sum_buf[kk] = total

        def across(h, zz):
            total = in_ref[part(h), chunk(zz, x)]
            for e in range(1, fast):
                arrived(x_buf.at[e - 1, zz, part(h)], x_r.at[h, e - 1, zz])
                total += x_buf[e - 1, zz, part(h)]
            return total

        def pass_on(h, zz, has_behind, buf, recv):
            work[part(h), chunk(zz, x)] = across(h, zz)

            @pl.when(has_behind)
            def _():
                arrived(buf.at[zz, part(h)], recv.at[h, zz])
                work[part(h), chunk(zz, x)] += buf[zz, part(h)]

        for d in range(slow - 1, 0, -1):
            for h in range(PARTS):
                when(z + d < slow, lambda: pass_on(h, z + d, has_down, up_buf, up_r))
                send(z + d < slow, lambda d=d, h=h: remote(
                    work.at[part(h), chunk(z + d, x)], up_buf.at[z + d, part(h)],
                    up_s.at[h, z + d], up_r.at[h, z + d], above))
                when(z - d >= 0, lambda: pass_on(h, z - d, has_up, down_buf, down_r))
                send(z - d >= 0, lambda d=d, h=h: remote(
                    work.at[part(h), chunk(z - d, x)], down_buf.at[z - d, part(h)],
                    down_s.at[h, z - d], down_r.at[h, z - d], below))
            for kk in range(per_block):
                if kk * (slow - 1) // per_block == slow - 1 - d:
                    when(at_root, lambda: settle(kk))
                    send(at_root & (which * per_block + kk != col_pos), lambda kk=kk: remote(
                        sum_buf.at[kk], late_buf, late_s.at[kk], late_r,
                        {"col": which * per_block + kk}))
        def close(h, buf, recv):
            arrived(buf.at[z, part(h)], recv.at[h, z])
            own[part(h), :] += buf[z, part(h)]

        for h in range(PARTS):
            own[part(h), :] = across(h, z)
            when(has_down, lambda: close(h, up_buf, up_r))
            when(has_up, lambda: close(h, down_buf, down_r))

        @pl.when(my_root != col_pos)
        def _():
            arrived(late_buf, late_r)
            own[...] += late_buf[...]

        @pl.when(my_root == col_pos)
        def _():
            own[...] += sum_buf[col_pos % per_block]

        mine = own[...] * inverse
    else:
        mine = in_ref[...]

    if gather:
        out_ref[:, chunk(z, x)] = mine

        def hand_on(h, zz, pred, upward, downward):
            there = out_ref.at[part(h), chunk(zz, x)]
            if upward is not None:
                send(upward, lambda: remote(there, there, gup_s.at[h, zz], gup_r.at[h, zz], above))
            if downward is not None:
                send(downward, lambda: remote(there, there, gdown_s.at[h, zz], gdown_r.at[h, zz], below))
            for e in range(1, fast):
                send(pred, lambda e=e: remote(
                    there, there, gx_s.at[h, e - 1, zz], gx_r.at[h, e - 1, zz], beside(e)))

        def to_column(h, zz, xx, pred):
            kk = zz * fast + xx - which * per_block
            wanted = at_root & ((zz * fast + xx) // per_block == which)
            if pred is not True:
                wanted = wanted & pred

            def place():
                out_ref[part(h), column(kk)] = out_ref[part(h), chunk(zz, xx)]

            for g in range(1, groups):
                send(wanted, lambda g=g: remote(
                    out_ref.at[part(h), chunk(zz, xx)], out_ref.at[part(h), column(kk)],
                    grow_s.at[h, g - 1, kk], gcol_r.at[h, kk], {"row": (group + g) % groups * 2 + core}))
            send(wanted, lambda: remote(
                out_ref.at[part(h), chunk(zz, xx)], out_ref.at[part(h), column(kk)],
                gcore_s.at[h, kk], gcol_r.at[h, kk], core_peer))
            when(wanted, place)

        def from_beside(h, zz, pred):
            for e in range(1, fast):
                xx = (x + fast - e) % fast
                when(pred, lambda: arrived(out_ref.at[part(h), chunk(zz, xx)], gx_r.at[h, e - 1, zz]))
                to_column(h, zz, xx, pred)

        for h in range(PARTS):
            hand_on(h, z, True, has_up, has_down)
            to_column(h, z, x, True)
        for d in range(1, slow):
            low, high = z - d, z + d
            for h in range(PARTS):
                when(low >= 0, lambda: arrived(out_ref.at[part(h), chunk(low, x)], gup_r.at[h, low]))
                hand_on(h, low, low >= 0, (low >= 0) & has_up, None)
                to_column(h, low, x, low >= 0)
                when(high < slow, lambda: arrived(out_ref.at[part(h), chunk(high, x)], gdown_r.at[h, high]))
                hand_on(h, high, high < slow, None, (high < slow) & has_down)
                to_column(h, high, x, high < slow)
                if d == 1:
                    from_beside(h, z, True)
                else:
                    from_beside(h, low + 1, low + 1 >= 0)
                    from_beside(h, high - 1, high - 1 < slow)
        for h in range(PARTS):
            from_beside(h, z - slow + 1, z - slow + 1 >= 0)
            from_beside(h, z + slow - 1, z + slow - 1 < slow)
        for kk in range(per_block):
            for h in range(PARTS):
                when(jnp.logical_not(at_root), lambda: arrived(
                    out_ref.at[part(h), column(kk)], gcol_r.at[h, kk]))
                send(relays, lambda kk=kk, h=h: remote(
                    out_ref.at[part(h), column(kk)], out_ref.at[part(h), column(kk)],
                    gcore_s.at[h, kk], gcol_r.at[h, kk], core_peer))
    else:
        out_ref[...] = mine
    for pred, make in sent:
        when(pred, lambda: make().wait_send())


def exchange(value, scatter, gather, n_row, n_col, width, inverse, collective_id):
    fast = 1
    while fast * fast * 4 <= n_col:
        fast *= 2
    slow = n_col // fast
    per_block = n_row
    dims = value.shape[0]
    f32 = jnp.float32
    dma = pltpu.SemaphoreType.DMA
    total = (n_col + per_block) * width
    scratch = []
    if scatter:
        piece = (dims, width)
        groups = n_row // 2
        scratch += [
            pltpu.VMEM((dims, n_col * width), f32),
            pltpu.VMEM(piece, f32),
            pltpu.VMEM((per_block,) + piece, f32),
            pltpu.VMEM((per_block,) + piece, f32),
            pltpu.VMEM((groups, per_block) + piece, f32),
            pltpu.VMEM((fast - 1, slow) + piece, f32),
            pltpu.VMEM((slow,) + piece, f32),
            pltpu.VMEM((slow,) + piece, f32),
            pltpu.VMEM(piece, f32), dma((per_block,)), dma,
            dma((per_block,)), dma((per_block,)), dma((per_block,)), dma((groups, per_block)),
            dma((PARTS, fast - 1, slow)), dma((PARTS, fast - 1, slow)),
            dma((PARTS, slow)), dma((PARTS, slow)), dma((PARTS, slow)), dma((PARTS, slow)),
        ]
    if gather:
        scratch += [
            dma((PARTS, slow)), dma((PARTS, slow)), dma((PARTS, slow)), dma((PARTS, slow)),
            dma((PARTS, fast - 1, slow)), dma((PARTS, fast - 1, slow)),
            dma((PARTS, max(n_row // 2 - 1, 1), per_block)), dma((PARTS, per_block)), dma((PARTS, per_block)),
        ]
    whole = pl.BlockSpec(memory_space=pltpu.VMEM)
    return pl.pallas_call(
        functools.partial(
            exchange_kernel, scatter, gather, n_row, n_col, slow, fast, width, inverse
        ),
        out_shape=jax.ShapeDtypeStruct((dims, total if gather else width), f32),
        in_specs=[whole],
        out_specs=whole,
        scratch_shapes=scratch,
        compiler_params=pltpu.CompilerParams(
            collective_id=collective_id, has_side_effects=True, vmem_limit_bytes=48 * 1024 * 1024
        ),
    )(value)


def local(coords, dissimilarity):
    n_row, n_col = lax.axis_size("row"), lax.axis_size("col")
    width = coords.shape[1]
    inverse = 1.0 / (width * n_row * n_col)
    trade = functools.partial(exchange, n_row=n_row, n_col=n_col, width=width, inverse=inverse)
    both = trade(coords, False, True, collective_id=0)
    for iteration in range(ITERS):
        parts = local_terms(both, dissimilarity, n_col // n_row)
        last = iteration == ITERS - 1
        both = trade(parts, True, not last, collective_id=1 + iteration)
    return both


def solution(mesh):
    in_specs = (P(None, ("row", "col")), P("row", "col"))
    out_specs = P(None, ("row", "col"))
    return jax.shard_map(local, mesh=mesh, in_specs=in_specs, out_specs=out_specs, check_vma=False)
```
